256 devices in a mesh: req: 4 (over x), blk: 64 (over z, y, core).
Axes of the slice: x: 4, y: 4, z: 8, core: 2. Of those that a mesh axis runs over, the one named last changes fastest.
Arguments:
- tokens: bfloat16 [4, 8192, 2048], P('req', 'blk'), may hold values from -6 to 6
- block_ids: int32 [4, 128], P('req', 'blk'), may hold values from 0 to 127, as said below
- lengths: int32 [4], P('req'), may hold values from 4097 to 8192, as said below
- page_table: int32 [4, 2, 128], P('req'), may hold values from 0 to 255, as said below
- qkv_weight: bfloat16 [2048, 3072], P(('req', 'blk')), may hold values from -0.125 to 0.125
- q_gain: float32 [256], replicated
- k_gain: float32 [256], replicated
Outputs:
- attended: bfloat16 [4, 8192, 2048], P('req', 'blk')
- kv_cache: bfloat16 [4, 256, 64, 512], P('req', 'blk')
The draws below stay inside these ranges and needn't reach their ends.
Inputs may be any that keep to these rules, and one draw needn't show every extreme that they name: `lengths`: one prompt has length exactly 8192. `block_ids`: the two entries of one device are b and 127 - b; over a prompt the first entries are a permutation of 0 to 63. `page_table`: each prompt's entries are a permutation of 0 to 255.
All inputs are finite; a program needn't handle non-finite values.
Results may differ from the reference program's by a relative error of at most 0.013.
The reference program's roundings to bfloat16 on the way count: a program that leaves them out, or rounds other values in their place, can miss the bound.
Values may be sent and summed in bfloat16 or wider, within the bound.
A program may use at most 128 MiB of HBM per device.

```python
import math
import jax
import jax.numpy as jnp
from jax import lax

D = 2048
H = 8
KVH = 2
HD = 256
BLK_ROWS = 64
SEQ = 8192
QKV = 3072
N_REQ = 4
N_BLK = 64


def draw_lengths(key, part):
    first_key = jax.random.fold_in(key, 101)
    second_key = jax.random.fold_in(key, 102)
    drawn = jax.random.randint(first_key, (N_REQ,), SEQ // 2 + 1, SEQ + 1)
    longest = jax.random.randint(second_key, (), 0, N_REQ)
    return jnp.where(jnp.arange(N_REQ) == longest, SEQ, drawn).astype(jnp.int32)


def draw_block_ids(key, part):
    base_key = jax.random.fold_in(key, 201)
    orders = jnp.stack([jax.random.permutation(jax.random.fold_in(base_key, request), N_BLK) for request in range(N_REQ)])
    paired = jnp.stack([orders, 2 * N_BLK - 1 - orders], -1)
    return paired.reshape(N_REQ, 2 * N_BLK).astype(jnp.int32)


def draw_page_table(key, part):
    base_key = jax.random.fold_in(key, 301)
    orders = jnp.stack([jax.random.permutation(jax.random.fold_in(base_key, request), KVH * 2 * N_BLK) for request in range(N_REQ)])
    return orders.reshape(N_REQ, KVH, 2 * N_BLK).astype(jnp.int32)


def gain_values(key):
    return jnp.exp(jax.random.uniform(key, (HD,), jnp.float32, jnp.log(0.28), jnp.log(0.56)))


def draw_q_gain(key, part):
    return gain_values(jax.random.fold_in(key, 401))


def draw_k_gain(key, part):
    return gain_values(jax.random.fold_in(key, 402))


def level_of(own_key, dims, pieces, least, top_value):
    loudness, own = 1.0, jax.random.fold_in(own_key, 6)
    for dim, parts in pieces:
        steps = jnp.exp(jax.random.uniform(jax.random.fold_in(own, dim), (parts,), jnp.float32, least / len(pieces), top_value / len(pieces)))
        loudness = loudness * jnp.repeat(steps, dims[dim] // parts).reshape([-1 if axis == dim else 1 for axis in range(len(dims))])
    return loudness


def bell_draw(key, extent, width, limit, split=(), held_as=jnp.bfloat16):
    values = width * jax.random.normal(key, extent, jnp.float32)
    if split:
        values = values * level_of(key, extent, split, -0.22, 0.18)
    return jnp.clip(values, -limit, limit).astype(held_as)


def setup_inputs(seed: int = 0) -> dict:
    splits = jax.random.split(jax.random.key(seed), 8)
    return {
        "tokens": bell_draw(splits[0], (N_REQ, SEQ, D), 1.0, 6.0, ((0, 4), (1, 64))),
        "block_ids": draw_block_ids(jax.random.fold_in(splits[7], 71), 0),
        "lengths": draw_lengths(jax.random.fold_in(splits[7], 71), 0),
        "page_table": draw_page_table(jax.random.fold_in(splits[7], 71), 0),
        "qkv_weight": bell_draw(splits[4], (D, QKV), D ** -0.5, 0.125, ((0, 256),)),
        "q_gain": draw_q_gain(jax.random.fold_in(splits[7], 71), 0),
        "k_gain": draw_k_gain(jax.random.fold_in(splits[7], 71), 0),
    }


ROPE_BASE = 1000000.0
NORM_EPS = 1e-06
FLOOR_SCORE = -1e+30

def head_norm(tensor, scale_gain):
    return tensor * lax.rsqrt(lax.optimization_barrier(jnp.mean(tensor * tensor, axis=-1, keepdims=True)) + NORM_EPS) * scale_gain

def rotary(tensor, positions):
    half_dim = tensor.shape[-1] // 2
    channel = jnp.arange(half_dim).astype(jnp.float32)
    inverse = jnp.power(jnp.float32(ROPE_BASE), -2.0 * channel / tensor.shape[-1])
    angles = positions.astype(jnp.float32)[:, None] * inverse[None, :]
    cosine = jnp.cos(angles)[:, None, :]
    sine_part = jnp.sin(angles)[:, None, :]
    front_half = tensor[..., :half_dim]
    second = tensor[..., half_dim:]
    return jnp.concatenate([front_half * cosine - second * sine_part, second * cosine + front_half * sine_part], -1)

def reference(tokens, block_ids, lengths, page_table, qkv_weight, q_gain, k_gain):
    groups = H // KVH
    query_block = math.gcd(SEQ, 512)
    block_total = SEQ // query_block
    attended_list = []
    cache_list = []
    for request in range(N_REQ):
        positions = (block_ids[request][:, None] * BLK_ROWS + jnp.arange(BLK_ROWS, dtype=jnp.int32)[None, :]).reshape(SEQ).astype(jnp.int32)
        projected = jnp.dot(tokens[request], qkv_weight, preferred_element_type=jnp.float32)
        query_raw = projected[:, :H * HD].reshape(SEQ, H, HD)
        key_raw = projected[:, H * HD:(H + KVH) * HD].reshape(SEQ, KVH, HD)
        value_raw = projected[:, (H + KVH) * HD:].reshape(SEQ, KVH, HD)
        queries = rotary(head_norm(query_raw, q_gain), positions).astype(jnp.bfloat16)
        key_rows = rotary(head_norm(key_raw, k_gain), positions).astype(jnp.bfloat16)
        values = head_norm(value_raw, 1.0).astype(jnp.bfloat16)
        length = lengths[request]
        grouped = lax.optimization_barrier(queries).astype(jnp.float32).reshape(SEQ, KVH, groups, HD)
        key_wide = lax.optimization_barrier(key_rows).astype(jnp.float32)
        value_wide = lax.optimization_barrier(values).astype(jnp.float32)
        key_live = positions < length

        def attend(block_number):
            query_rows = lax.dynamic_slice_in_dim(grouped, block_number * query_block, query_block, 0)
            query_pos = lax.dynamic_slice_in_dim(positions, block_number * query_block, query_block, 0)
            scores = jnp.einsum('rgad,kgd->rgak', query_rows, key_wide)
            allowed = ((positions[None, :] <= query_pos[:, None]) & key_live[None, :])[:, None, None, :]
            row_max = lax.optimization_barrier(jnp.max(jnp.where(allowed, scores, FLOOR_SCORE), -1, keepdims=True))
            weights = jnp.where(allowed, jnp.exp(scores - row_max), 0.0)
            row_sum = lax.optimization_barrier(jnp.sum(weights, -1))
            rounded = lax.optimization_barrier(weights.astype(jnp.bfloat16)).astype(jnp.float32)
            summed = jnp.einsum('rgak,kgd->rgad', rounded, value_wide)
            query_live = query_pos < length
            divisor = jnp.where(query_live[:, None, None], row_sum, 1.0)
            result = jnp.where(query_live[:, None, None, None], summed / divisor[..., None], 0.0)
            return result.reshape(query_block, H * HD).astype(jnp.bfloat16)
        attended_list.append(lax.map(attend, jnp.arange(block_total)).reshape(SEQ, H * HD))
        kv_rows = jnp.concatenate([key_rows, values], -1)
        kv_rows = jnp.where(key_live[:, None, None], kv_rows, jnp.zeros_like(kv_rows))
        ordered = jnp.zeros_like(kv_rows).at[positions].set(kv_rows)
        page_rows = ordered.reshape(2 * N_BLK, BLK_ROWS, KVH, 2 * HD).transpose(2, 0, 1, 3).reshape(KVH * 2 * N_BLK, BLK_ROWS, 2 * HD)
        cache_list.append(jnp.zeros_like(page_rows).at[page_table[request].reshape(-1).astype(jnp.int32)].set(page_rows))
    return (jnp.stack(attended_list), jnp.stack(cache_list))
```

```python
import jax
import jax.numpy as jnp
from jax import lax
from jax.experimental import pallas as pl
from jax.experimental.pallas import tpu as pltpu
from jax.sharding import PartitionSpec as P

H = 8
KVH = 2
HD = 256
GRP = H // KVH
ROPE_BASE = 1000000.0
NORM_EPS = 1e-06
FLOOR_SCORE = -1e30
MESH = pl.DeviceIdType.MESH

NX, NY, NZ = 4, 4, 8
ROWS = 128
UNIT = 2 * ROWS + 16
CUTS = ((0, ROWS + 16), (ROWS + 16, ROWS))
STEPS = 16
T_FWD = 4
T_ATT = 9

OFFS = {"x": (1, 3, 2), "y": (1, 3, 2), "z": (1, 7, 2, 6, 3, 5, 4)}
SIZE = {"x": NX, "y": NY, "z": NZ}


def kernel(
    tok, meta, ids, w, qg, kg, tpos, length,
    out, pages,
    tokb, metab, idb, wtmp, wk, wv, wq, own, buf, qb, mb, lb, acc, pacc,
    osend, orecv, psend, precv,
    s_sib, r_sib, s_w, r_w, s_qx, r_qx, s_ring, r_ring, s_loc,
):
    r = lax.axis_index("req")
    b = lax.axis_index("blk")
    c = b % 2
    y = (b // 2) % NY
    z = b // (2 * NY)

    def dev(x_, y_, z_):
        return (x_, (z_ * NY + y_) * 2 + c)

    sib = (r, b + 1 - 2 * c)
    here = {"x": r, "y": y, "z": z}

    def along(ax, k):
        at = dict(here)
        at[ax] = (here[ax] + k) % SIZE[ax]
        return dev(at["x"], at["y"], at["z"])

    barrier = pltpu.get_barrier_semaphore()
    partners = [sib] + [along(ax, k) for ax in "xyz" for k in OFFS[ax]]
    for d in partners:
        pl.semaphore_signal(barrier, inc=1, device_id=d, device_id_type=MESH)
    pl.semaphore_wait(barrier, len(partners))

    def remote(src, dst, ss, rs, d):
        return pltpu.make_async_remote_copy(
            src_ref=src, dst_ref=dst, send_sem=ss, recv_sem=rs, device_id=d, device_id_type=MESH
        )

    mine = pl.ds(pl.multiple_of(c * ROWS, ROWS), ROWS)
    other = pl.ds(pl.multiple_of((1 - c) * ROWS, ROWS), ROWS)
    swap = [
        (w.at[1 - c], wtmp, wtmp),
        (tok, tokb.at[mine], tokb.at[other]),
        (meta, metab.at[mine], metab.at[other]),
        (ids, idb.at[c], idb.at[1 - c]),
    ]
    sends = []
    for i, (src, dst, _) in enumerate(swap):
        cp = remote(src, dst, s_sib.at[i], r_sib.at[i], sib)
        cp.start()
        sends.append(cp)

    def sib_recv(i):
        src, _, arrives = swap[i]
        remote(src, arrives, s_sib.at[i], r_sib.at[i], sib).wait_recv()

    local = [
        pltpu.make_async_copy(tok, tokb.at[mine], s_loc.at[0]),
        pltpu.make_async_copy(meta, metab.at[mine], s_loc.at[1]),
        pltpu.make_async_copy(ids, idb.at[c], s_loc.at[2]),
    ]
    for cp in local:
        cp.start()

    sib_recv(0)
    w_own = w[c].astype(jnp.float32)
    w_sib = wtmp[...].astype(jnp.float32)
    first = c == 0
    rows16 = jnp.concatenate(
        [jnp.where(first, w_own, w_sib), jnp.where(first, w_sib, w_own)], axis=0
    ).astype(jnp.bfloat16)
    wk[r, z, y] = rows16[:, :HD]
    wv[r, z, y] = rows16[:, HD : 2 * HD]
    wq[r, z, y] = rows16[:, 2 * HD :]

    def region(done, at):
        return tuple(slice(None) if ax in done else at[ax] for ax in "xzy")

    def phase(number, wb, done, ax):
        pairs = []
        for k, off in enumerate(OFFS[ax]):
            came = dict(here)
            came[ax] = (here[ax] - off + SIZE[ax]) % SIZE[ax]
            src = wb.at[region(done, here)]
            ss, rs, d = s_w.at[number, k], r_w.at[number, k], along(ax, off)
            pairs.append(
                (remote(src, src, ss, rs, d), remote(src, wb.at[region(done, came)], ss, rs, d))
            )
        for cp, _ in pairs:
            cp.start()
            sends.append(cp)
        return [arrive for _, arrive in pairs]

    def arrived(copies):
        for cp in copies:
            cp.wait_recv()

    k1 = phase(0, wk, "", "z")
    v1 = phase(1, wv, "", "z")
    q1 = phase(2, wq, "", "y")
    arrived(k1)
    k2 = phase(3, wk, "z", "y")
    arrived(v1)
    v2 = phase(4, wv, "z", "x")
    arrived(q1)
    q2 = phase(5, wq, "y", "z")
    arrived(k2)
    k3 = phase(6, wk, "zy", "x")
    arrived(v2)
    v3 = phase(7, wv, "zx", "y")

    mb[...] = jnp.full_like(mb, FLOOR_SCORE)
    lb[...] = jnp.zeros_like(lb)
    acc[...] = jnp.zeros_like(acc)
    pacc[...] = jnp.zeros_like(pacc)
    for i in (1, 2, 3):
        sib_recv(i)
    for cp in local:
        cp.wait()

    def normed(u, gain):
        scaled = u * lax.rsqrt(jnp.mean(u * u, axis=-1, keepdims=True) + NORM_EPS)
        return scaled if gain is None else scaled * gain[...]

    def rotated(u):
        half = HD // 2
        cosine = metab[:, :half]
        sine = metab[:, half : 2 * half]
        front, second = u[:, :half], u[:, half:]
        return jnp.concatenate(
            [front * cosine - second * sine, second * cosine + front * sine], axis=-1
        )

    def project(weights):
        return jnp.dot(
            tokb[...],
            weights.reshape(NX * NY * NZ * 16, HD),
            preferred_element_type=jnp.float32,
        )

    arrived(k3)
    keys = rotated(normed(project(wk[...]), kg)).astype(jnp.bfloat16)
    for i in range(2):
        own[i, :ROWS] = keys[i * ROWS : (i + 1) * ROWS]
        own[i, ROWS : ROWS + 16] = jnp.concatenate([idb[i], idb[i]], axis=-1)
    arrived(v3)
    values = normed(project(wv[...]), None).astype(jnp.bfloat16)
    for i in range(2):
        own[i, ROWS + 16 :] = values[i * ROWS : (i + 1) * ROWS]

    turn = y == (NY - 1 - z + NZ) % NY
    back = y == (NY - z + NZ) % NY

    def pick(cond, one, two):
        return tuple(jnp.where(cond, i, j) for i, j in zip(one, two))

    zp, zm, yp, ym = along("z", 1), along("z", NZ - 1), along("y", 1), along("y", NY - 1)
    to = [pick(turn, zp, yp), pick(back, zm, ym), pick(turn, yp, zp), pick(back, ym, zm)]

    def ring_copy(s, j, t, src):
        piece = pl.ds(*CUTS[j])
        return remote(
            src.at[piece], buf.at[s, t, piece], s_ring.at[s, t, j], r_ring.at[s, t, j], to[s]
        )

    for j in range(len(CUTS)):
        for s in range(4):
            ring_copy(s, j, 0, own.at[s // 2]).start()

    def ring_step(t):
        for j in range(len(CUTS)):
            for s in range(4):
                ring_copy(s, j, t, own.at[s // 2]).wait_recv()
                if s % 2 == 0:
                    ring_copy(s, j, t + 1, buf.at[s, t]).start()
                else:

                    @pl.when(t < STEPS - 2)
                    def _():
                        ring_copy(s, j, t + 1, buf.at[s, t]).start()

    def repeat(lo, hi, f):
        def go(t, carry):
            f(t)
            return carry

        lax.fori_loop(lo, hi, go, 0)

    halves = (pl.ds(0, NZ // 2), pl.ds(NZ // 2, NZ // 2))
    arrived(q2)
    nxt, prv = along("x", 1), along("x", NX - 1)
    x_prv, x_nxt, x_far = (r + NX - 1) % NX, (r + 1) % NX, (r + 2) % NX

    def q_copy(n, plane, half, d):
        ref = wq.at[plane, halves[half]]
        return remote(ref, ref, s_qx.at[n], r_qx.at[n], d)

    hop1 = [q_copy(0, r, 0, nxt), q_copy(1, r, 1, prv), q_copy(2, r, 1, nxt), q_copy(3, r, 0, prv)]
    for cp in hop1:
        cp.start()
        sends.append(cp)
    repeat(0, T_FWD, ring_step)
    arrived([q_copy(0, x_prv, 0, nxt), q_copy(1, x_nxt, 1, prv)])
    for cp in (q_copy(4, x_prv, 0, nxt), q_copy(5, x_nxt, 1, prv)):
        cp.start()
        sends.append(cp)
    repeat(T_FWD, T_ATT, ring_step)
    arrived(
        [
            q_copy(2, x_prv, 1, nxt),
            q_copy(3, x_nxt, 0, prv),
            q_copy(4, x_far, 0, nxt),
            q_copy(5, x_far, 1, prv),
        ]
    )

    def project_head(h):
        cols = pl.ds(pl.multiple_of(h * HD, HD), HD)
        rows = pl.ds(pl.multiple_of(h * 2 * ROWS, 2 * ROWS), 2 * ROWS)
        qb[rows, :] = rotated(normed(project(wq[:, :, :, :, cols]), qg)).astype(jnp.bfloat16)

    repeat(0, GRP, project_head)

    limit = length[0].astype(jnp.float32)
    lane = lax.broadcasted_iota(jnp.int32, (1, ROWS), 1)
    lane_in_block = (lane % (ROWS // 2)).astype(jnp.float32)

    def attend(units):
        key_pos = []
        for u in units:
            number = u[ROWS : ROWS + 16, :ROWS].astype(jnp.float32)[:1]
            key_pos.append(number * (ROWS // 2) + lane_in_block)
        seen = [jnp.where(kp < limit, kp, 1e9) for kp in key_pos]
        keys = jnp.concatenate([u[:ROWS] for u in units], axis=0)
        values = jnp.concatenate([u[ROWS + 16 :] for u in units], axis=0)

        def head(h):
            rows = pl.ds(pl.multiple_of(h * 2 * ROWS, 2 * ROWS), 2 * ROWS)
            query_pos = metab[:, HD : HD + ROWS]
            scores = lax.dot_general(
                qb[rows, :], keys, (((1,), (1,)), ((), ())), preferred_element_type=jnp.float32
            )
            parts = [
                jnp.where(sn <= query_pos, scores[:, i * ROWS : (i + 1) * ROWS], FLOOR_SCORE)
                for i, sn in enumerate(seen)
            ]
            old_max = mb[rows, :]
            top = parts[0]
            for part in parts[1:]:
                top = jnp.maximum(top, part)
            new_max = jnp.maximum(old_max, jnp.max(top, axis=-1, keepdims=True))
            rescale = jnp.exp(old_max - new_max)
            weights = [jnp.exp(part - new_max) for part in parts]
            total = weights[0]
            for wt in weights[1:]:
                total = total + wt
            mb[rows, :] = new_max
            lb[rows, :] = lb[rows, :] * rescale + total
            product = jnp.dot(
                jnp.concatenate([wt.astype(jnp.bfloat16) for wt in weights], axis=-1),
                values,
                preferred_element_type=jnp.float32,
            )
            acc[rows, :] = acc[rows, :] * jnp.concatenate([rescale, rescale], axis=-1) + product

        repeat(0, GRP, head)

        def page_part(i):
            rows = pl.ds(pl.multiple_of(i * 2 * ROWS, 2 * ROWS), 2 * ROWS)
            wanted = tpos[rows, :]
            chosen = jnp.concatenate(
                [jnp.where(wanted == kp, 1.0, 0.0).astype(jnp.bfloat16) for kp in key_pos], axis=-1
            )
            pacc[rows, :HD] += jnp.dot(chosen, keys, preferred_element_type=jnp.float32)
            pacc[rows, HD:] += jnp.dot(chosen, values, preferred_element_type=jnp.float32)

        repeat(0, 2, page_part)

    def attend_step(i):
        attend([buf[s, i] for s in range(4)])

    def both(t):
        ring_step(t)
        attend_step(2 * (t - T_ATT))
        attend_step(2 * (t - T_ATT) + 1)

    repeat(T_ATT, STEPS - 1, both)
    repeat(2 * (STEPS - 1 - T_ATT), STEPS - 1, attend_step)
    for j in range(len(CUTS)):
        for s in (0, 2):
            ring_copy(s, j, STEPS - 1, own.at[s // 2]).wait_recv()
    attend([own[0], own[1], buf[0, STEPS - 1], buf[2, STEPS - 1]])

    def result(part, h):
        start = h * 2 * ROWS + part * ROWS
        rows = pl.ds(pl.multiple_of(start, ROWS), ROWS)
        live = metab[pl.ds(pl.multiple_of(part * ROWS, ROWS), ROWS), HD : HD + 1] < limit
        total = jnp.sum(lb[rows, :], axis=-1, keepdims=True)
        divided = acc[rows, :] / jnp.where(live, total, 1.0)
        return jnp.where(live, divided, 0.0).astype(jnp.bfloat16)

    for h in range(GRP):
        osend[:, h * HD : (h + 1) * HD] = result(1 - c, h)
    o_cp = remote(osend, orecv, s_sib.at[4], r_sib.at[4], sib)
    o_cp.start()
    half = 4 * 64
    theirs = pl.ds(pl.multiple_of((1 - c) * half, half), half)
    psend[...] = pacc[theirs, :].astype(jnp.bfloat16)
    p_cp = remote(psend, precv, s_sib.at[5], r_sib.at[5], sib)
    p_cp.start()
    my_cols = pl.multiple_of(c * GRP * HD, GRP * HD)
    for h in range(GRP):
        out[:, pl.ds(my_cols + h * HD, HD)] = result(c, h)
    p_cp.wait()
    ours = pl.ds(pl.multiple_of(c * half, half), half)
    pages[...] = (pacc[ours, :] + precv[...].astype(jnp.float32)).astype(jnp.bfloat16)
    o_cp.wait()
    out[:, pl.ds(pl.multiple_of((1 - c) * GRP * HD, GRP * HD), GRP * HD)] = orecv[...]

    for cp in sends:
        cp.wait_send()

    def ring_sent(t):
        for j in range(len(CUTS)):
            for s in range(4):
                if s % 2 == 0:
                    ring_copy(s, j, t, own.at[s // 2]).wait_send()
                else:

                    @pl.when(t < STEPS - 1)
                    def _():
                        ring_copy(s, j, t, own.at[s // 2]).wait_send()

    repeat(0, STEPS, ring_sent)


def body(tokens, block_ids, lengths, page_table, qkv_weight, q_gain, k_gain):
    own_ids = block_ids[0]
    blk_rows = ROWS // 2
    positions = (
        own_ids[:, None] * blk_rows + jnp.arange(blk_rows, dtype=jnp.int32)[None, :]
    ).reshape(ROWS)
    half = HD // 2
    channel = jnp.arange(half).astype(jnp.float32)
    inverse = jnp.power(jnp.float32(ROPE_BASE), -2.0 * channel / HD)
    pos_f = positions.astype(jnp.float32)
    angles = pos_f[:, None] * inverse[None, :]
    meta = jnp.concatenate(
        [jnp.cos(angles), jnp.sin(angles), jnp.broadcast_to(pos_f[:, None], (ROWS, ROWS))], axis=-1
    )
    ids = jnp.broadcast_to(
        jnp.repeat(own_ids, blk_rows).astype(jnp.bfloat16)[None, :], (16, ROWS)
    )
    blk = lax.axis_index("blk")
    core = blk % 2
    w = jnp.stack(
        [
            jnp.concatenate(
                [
                    qkv_weight[:, H * HD + g * HD : H * HD + (g + 1) * HD],
                    qkv_weight[:, (H + KVH + g) * HD : (H + KVH + g + 1) * HD],
                    qkv_weight[:, g * GRP * HD : (g + 1) * GRP * HD],
                ],
                axis=-1,
            )
            for g in range(KVH)
        ]
    )
    my_slots = (blk // 2) * 8 + jnp.arange(8, dtype=jnp.int32)
    table = lax.dynamic_index_in_dim(page_table[0], core, 0, keepdims=False)
    match = table[None, :] == my_slots[:, None]
    block_no = jnp.sum(
        jnp.where(match, jnp.arange(table.shape[0], dtype=jnp.int32)[None, :] + 1, 0), axis=1
    ) - 1
    wanted = block_no[:, None] * blk_rows + jnp.arange(blk_rows, dtype=jnp.int32)[None, :]
    wanted = jnp.where((block_no[:, None] >= 0) & (wanted < lengths[0]), wanted, -1)
    tpos = jnp.broadcast_to(
        wanted.reshape(8 * blk_rows, 1).astype(jnp.float32), (8 * blk_rows, ROWS)
    )

    vm = pl.BlockSpec(memory_space=pltpu.VMEM)
    dma = pltpu.SemaphoreType.DMA
    bf, f32 = jnp.bfloat16, jnp.float32
    attended, cache = pl.pallas_call(
        kernel,
        out_shape=(
            jax.ShapeDtypeStruct((ROWS, H * HD), bf),
            jax.ShapeDtypeStruct((4 * 64, 2 * HD), bf),
        ),
        in_specs=[vm] * 7 + [pl.BlockSpec(memory_space=pltpu.SMEM)],
        out_specs=(vm, vm),
        scratch_shapes=[
            pltpu.VMEM((2 * ROWS, 2048), bf),
            pltpu.VMEM((2 * ROWS, 3 * ROWS), f32),
            pltpu.VMEM((2, 16, ROWS), bf),
            pltpu.VMEM((8, 6 * HD), bf),
            pltpu.VMEM((NX, NZ, NY, 16, HD), bf),
            pltpu.VMEM((NX, NZ, NY, 16, HD), bf),
            pltpu.VMEM((NX, NZ, NY, 16, GRP * HD), bf),
            pltpu.VMEM((2, UNIT, HD), bf),
            pltpu.VMEM((4, STEPS, UNIT, HD), bf),
            pltpu.VMEM((GRP * 2 * ROWS, HD), bf),
            pltpu.VMEM((GRP * 2 * ROWS, ROWS), f32),
            pltpu.VMEM((GRP * 2 * ROWS, ROWS), f32),
            pltpu.VMEM((GRP * 2 * ROWS, HD), f32),
            pltpu.VMEM((8 * 64, 2 * HD), f32),
            pltpu.VMEM((ROWS, GRP * HD), bf),
            pltpu.VMEM((ROWS, GRP * HD), bf),
            pltpu.VMEM((4 * 64, 2 * HD), bf),
            pltpu.VMEM((4 * 64, 2 * HD), bf),
            dma((6,)),
            dma((6,)),
            dma((8, 7)),
            dma((8, 7)),
            dma((6,)),
            dma((6,)),
            dma((4, STEPS, len(CUTS))),
            dma((4, STEPS, len(CUTS))),
            dma((3,)),
        ],
        compiler_params=pltpu.CompilerParams(
            collective_id=0, has_side_effects=True, vmem_limit_bytes=56 << 20
        ),
        name="prefill",
    )(
        tokens[0],
        meta,
        ids,
        w,
        q_gain.reshape(1, HD),
        k_gain.reshape(1, HD),
        tpos,
        lengths,
    )
    return (attended[None], cache.reshape(1, 4, 64, 2 * HD))


def solution(mesh):
    in_specs = (
        P("req", "blk", None),
        P("req", "blk"),
        P("req"),
        P("req", None, None),
        P(("req", "blk"), None),
        P(),
        P(),
    )
    out_specs = (P("req", "blk", None), P("req", "blk", None, None))
    return jax.shard_map(body, mesh=mesh, in_specs=in_specs, out_specs=out_specs, check_vma=False)
```

```python
import jax
import jax.numpy as jnp
from jax import lax
from jax.experimental import pallas as pl
from jax.experimental.pallas import tpu as pltpu
from jax.sharding import PartitionSpec as P

H = 8
KVH = 2
HD = 256
GRP = H // KVH
ROPE_BASE = 1000000.0
NORM_EPS = 1e-06
FLOOR_SCORE = -1e30
MESH = pl.DeviceIdType.MESH

NX, NY, NZ = 4, 4, 8
ROWS = 128
UNIT = 2 * ROWS + 16
CUTS = ((0, ROWS + 16), (ROWS + 16, ROWS))
STEPS = 16
T_FWD = 4
T_ATT = 9

OFFS = {"x": (1, 3, 2), "y": (1, 3, 2), "z": (1, 7, 2, 6, 3, 5, 4)}
SIZE = {"x": NX, "y": NY, "z": NZ}


def kernel(
    tok, meta, ids, w, qg, kg, tpos, length,
    out, pages,
    tokb, metab, idb, wtmp, wk, wv, wq, own, buf, qb, mb, lb, acc, pacc,
    osend, orecv, psend, precv,
    s_sib, r_sib, s_w, r_w, s_qx, r_qx, s_ring, r_ring, s_loc,
):
    r = lax.axis_index("req")
    b = lax.axis_index("blk")
    c = b % 2
    y = (b // 2) % NY
    z = b // (2 * NY)

    def dev(x_, y_, z_):
        return (x_, (z_ * NY + y_) * 2 + c)

    sib = (r, b + 1 - 2 * c)
    here = {"x": r, "y": y, "z": z}

    def along(ax, k):
        at = dict(here)
        at[ax] = (here[ax] + k) % SIZE[ax]
        return dev(at["x"], at["y"], at["z"])

    barrier = pltpu.get_barrier_semaphore()
    partners = [sib] + [along(ax, k) for ax in "xyz" for k in OFFS[ax]]
    for d in partners:
        pl.semaphore_signal(barrier, inc=1, device_id=d, device_id_type=MESH)
    pl.semaphore_wait(barrier, len(partners))

    def remote(src, dst, ss, rs, d):
        return pltpu.make_async_remote_copy(
            src_ref=src, dst_ref=dst, send_sem=ss, recv_sem=rs, device_id=d, device_id_type=MESH
        )

    mine = pl.ds(pl.multiple_of(c * ROWS, ROWS), ROWS)
    other = pl.ds(pl.multiple_of((1 - c) * ROWS, ROWS), ROWS)
    swap = [
        (w.at[1 - c], wtmp, wtmp),
        (tok, tokb.at[mine], tokb.at[other]),
        (meta, metab.at[mine], metab.at[other]),
        (ids, idb.at[c], idb.at[1 - c]),
    ]
    sends = []
    for i, (src, dst, _) in enumerate(swap):
        cp = remote(src, dst, s_sib.at[i], r_sib.at[i], sib)
        cp.start()
        sends.append(cp)

    def sib_recv(i):
        src, _, arrives = swap[i]
        remote(src, arrives, s_sib.at[i], r_sib.at[i], sib).wait_recv()

    local = [
        pltpu.make_async_copy(tok, tokb.at[mine], s_loc.at[0]),
        pltpu.make_async_copy(meta, metab.at[mine], s_loc.at[1]),
        pltpu.make_async_copy(ids, idb.at[c], s_loc.at[2]),
    ]
    for cp in local:
        cp.start()

    sib_recv(0)
    w_own = w[c].astype(jnp.float32)
    w_sib = wtmp[...].astype(jnp.float32)
    first = c == 0
    rows16 = jnp.concatenate(
        [jnp.where(first, w_own, w_sib), jnp.where(first, w_sib, w_own)], axis=0
    ).astype(jnp.bfloat16)
    wk[r, z, y] = rows16[:, :HD]
    wv[r, z, y] = rows16[:, HD : 2 * HD]
    wq[r, z, y] = rows16[:, 2 * HD :]

    def region(done, at):
        return tuple(slice(None) if ax in done else at[ax] for ax in "xzy")

    def phase(number, wb, done, ax):
        pairs = []
        for k, off in enumerate(OFFS[ax]):
            came = dict(here)
            came[ax] = (here[ax] - off + SIZE[ax]) % SIZE[ax]
            src = wb.at[region(done, here)]
            ss, rs, d = s_w.at[number, k], r_w.at[number, k], along(ax, off)
            pairs.append(
                (remote(src, src, ss, rs, d), remote(src, wb.at[region(done, came)], ss, rs, d))
            )
        for cp, _ in pairs:
            cp.start()
            sends.append(cp)
        return [arrive for _, arrive in pairs]

    def arrived(copies):
        for cp in copies:
            cp.wait_recv()

    k1 = phase(0, wk, "", "z")
    v1 = phase(1, wv, "", "z")
    q1 = phase(2, wq, "", "y")
    arrived(k1)
    k2 = phase(3, wk, "z", "y")
    arrived(v1)
    v2 = phase(4, wv, "z", "x")
    arrived(q1)
    q2 = phase(5, wq, "y", "z")
    arrived(k2)
    k3 = phase(6, wk, "zy", "x")
    arrived(v2)
    v3 = phase(7, wv, "zx", "y")

    mb[...] = jnp.full_like(mb, FLOOR_SCORE)
    lb[...] = jnp.zeros_like(lb)
    acc[...] = jnp.zeros_like(acc)
    pacc[...] = jnp.zeros_like(pacc)
    for i in (1, 2, 3):
        sib_recv(i)
    for cp in local:
        cp.wait()

    def normed(u, gain):
        scaled = u * lax.rsqrt(jnp.mean(u * u, axis=-1, keepdims=True) + NORM_EPS)
        return scaled if gain is None else scaled * gain[...]

    def rotated(u):
        half = HD // 2
        cosine = metab[:, :half]
        sine = metab[:, half : 2 * half]
        front, second = u[:, :half], u[:, half:]
        return jnp.concatenate(
            [front * cosine - second * sine, second * cosine + front * sine], axis=-1
        )

    def project(weights):
        return jnp.dot(
            tokb[...],
            weights.reshape(NX * NY * NZ * 16, HD),
            preferred_element_type=jnp.float32,
        )

    arrived(k3)
    keys = rotated(normed(project(wk[...]), kg)).astype(jnp.bfloat16)
    for i in range(2):
        own[i, :ROWS] = keys[i * ROWS : (i + 1) * ROWS]
        own[i, ROWS : ROWS + 16] = jnp.concatenate([idb[i], idb[i]], axis=-1)
    arrived(v3)
    values = normed(project(wv[...]), None).astype(jnp.bfloat16)
    for i in range(2):
        own[i, ROWS + 16 :] = values[i * ROWS : (i + 1) * ROWS]

    turn = y == (NY - 1 - z + NZ) % NY
    back = y == (NY - z + NZ) % NY

    def pick(cond, one, two):
        return tuple(jnp.where(cond, i, j) for i, j in zip(one, two))

    zp, zm, yp, ym = along("z", 1), along("z", NZ - 1), along("y", 1), along("y", NY - 1)
    to = [pick(turn, zp, yp), pick(back, zm, ym), pick(turn, yp, zp), pick(back, ym, zm)]

    def ring_copy(s, j, t, src):
        piece = pl.ds(*CUTS[j])
        return remote(
            src.at[piece], buf.at[s, t, piece], s_ring.at[s, t, j], r_ring.at[s, t, j], to[s]
        )

    for j in range(len(CUTS)):
        for s in range(4):
            ring_copy(s, j, 0, own.at[s // 2]).start()

    def ring_step(t):
        for j in range(len(CUTS)):
            for s in range(4):
                ring_copy(s, j, t, own.at[s // 2]).wait_recv()
                if s % 2 == 0:
                    ring_copy(s, j, t + 1, buf.at[s, t]).start()
                else:

                    @pl.when(t < STEPS - 2)
                    def _():
                        ring_copy(s, j, t + 1, buf.at[s, t]).start()

    def repeat(lo, hi, f):
        def go(t, carry):
            f(t)
            return carry

        lax.fori_loop(lo, hi, go, 0)

    halves = (pl.ds(0, NZ // 2), pl.ds(NZ // 2, NZ // 2))
    arrived(q2)
    nxt, prv = along("x", 1), along("x", NX - 1)
    x_prv, x_nxt, x_far = (r + NX - 1) % NX, (r + 1) % NX, (r + 2) % NX

    def q_copy(n, plane, half, d):
        ref = wq.at[plane, halves[half]]
        return remote(ref, ref, s_qx.at[n], r_qx.at[n], d)

    hop1 = [q_copy(0, r, 0, nxt), q_copy(1, r, 1, prv), q_copy(2, r, 1, nxt), q_copy(3, r, 0, prv)]
    for cp in hop1:
        cp.start()
        sends.append(cp)
    repeat(0, T_FWD, ring_step)
    arrived([q_copy(0, x_prv, 0, nxt), q_copy(1, x_nxt, 1, prv)])
    for cp in (q_copy(4, x_prv, 0, nxt), q_copy(5, x_nxt, 1, prv)):
        cp.start()
        sends.append(cp)
    repeat(T_FWD, T_ATT, ring_step)
    arrived(
        [
            q_copy(2, x_prv, 1, nxt),
            q_copy(3, x_nxt, 0, prv),
            q_copy(4, x_far, 0, nxt),
            q_copy(5, x_far, 1, prv),
        ]
    )

    def project_head(h):
        cols = pl.ds(pl.multiple_of(h * HD, HD), HD)
        rows = pl.ds(pl.multiple_of(h * 2 * ROWS, 2 * ROWS), 2 * ROWS)
        qb[rows, :] = rotated(normed(project(wq[:, :, :, :, cols]), qg)).astype(jnp.bfloat16)

    repeat(0, GRP, project_head)

    limit = length[0].astype(jnp.float32)
    lane = lax.broadcasted_iota(jnp.int32, (1, ROWS), 1)
    lane_in_block = (lane % (ROWS // 2)).astype(jnp.float32)

    def attend(units):
        key_pos = []
        for u in units:
            number = u[ROWS : ROWS + 16, :ROWS].astype(jnp.float32)[:1]
            key_pos.append(number * (ROWS // 2) + lane_in_block)
        seen = [jnp.where(kp < limit, kp, 1e9) for kp in key_pos]
        keys = jnp.concatenate([u[:ROWS] for u in units], axis=0)
        values = jnp.concatenate([u[ROWS + 16 :] for u in units], axis=0)

        def head(h):
            rows = pl.ds(h * 2 * ROWS, 2 * ROWS)
            query_pos = metab[:, HD : HD + ROWS]
            scores = lax.dot_general(
                qb[rows, :], keys, (((1,), (1,)), ((), ())), preferred_element_type=jnp.float32
            )
            parts = [
                jnp.where(sn <= query_pos, scores[:, i * ROWS : (i + 1) * ROWS], FLOOR_SCORE)
                for i, sn in enumerate(seen)
            ]
            old_max = mb[rows, :]
            top = parts[0]
            for part in parts[1:]:
                top = jnp.maximum(top, part)
            new_max = jnp.maximum(old_max, jnp.max(top, axis=-1, keepdims=True))
            rescale = jnp.exp(old_max - new_max)
            weights = [jnp.exp(part - new_max) for part in parts]
            total = weights[0]
            for wt in weights[1:]:
                total = total + wt
            mb[rows, :] = new_max
            lb[rows, :] = lb[rows, :] * rescale + total
            product = jnp.dot(
                jnp.concatenate([wt.astype(jnp.bfloat16) for wt in weights], axis=-1),
                values,
                preferred_element_type=jnp.float32,
            )
            acc[rows, :] = acc[rows, :] * jnp.concatenate([rescale, rescale], axis=-1) + product

        for h in range(GRP):
            head(h)

        def page_part(i):
            rows = pl.ds(pl.multiple_of(i * 2 * ROWS, 2 * ROWS), 2 * ROWS)
            wanted = tpos[rows, :]
            chosen = jnp.concatenate(
                [jnp.where(wanted == kp, 1.0, 0.0).astype(jnp.bfloat16) for kp in key_pos], axis=-1
            )
            pacc[rows, :HD] += jnp.dot(chosen, keys, preferred_element_type=jnp.float32)
            pacc[rows, HD:] += jnp.dot(chosen, values, preferred_element_type=jnp.float32)

        for i in range(2):
            page_part(i)

    def attend_step(i):
        attend([buf[s, i] for s in range(4)])

    def both(t):
        ring_step(t)
        attend_step(2 * (t - T_ATT))
        attend_step(2 * (t - T_ATT) + 1)

    repeat(T_ATT, STEPS - 1, both)
    repeat(2 * (STEPS - 1 - T_ATT), STEPS - 1, attend_step)
    for j in range(len(CUTS)):
        for s in (0, 2):
            ring_copy(s, j, STEPS - 1, own.at[s // 2]).wait_recv()
    attend([own[0], own[1], buf[0, STEPS - 1], buf[2, STEPS - 1]])

    def result(part, h):
        start = h * 2 * ROWS + part * ROWS
        rows = pl.ds(pl.multiple_of(start, ROWS), ROWS)
        live = metab[pl.ds(pl.multiple_of(part * ROWS, ROWS), ROWS), HD : HD + 1] < limit
        total = jnp.sum(lb[rows, :], axis=-1, keepdims=True)
        divided = acc[rows, :] / jnp.where(live, total, 1.0)
        return jnp.where(live, divided, 0.0).astype(jnp.bfloat16)

    for h in range(GRP):
        osend[:, h * HD : (h + 1) * HD] = result(1 - c, h)
    o_cp = remote(osend, orecv, s_sib.at[4], r_sib.at[4], sib)
    o_cp.start()
    half = 4 * 64
    theirs = pl.ds(pl.multiple_of((1 - c) * half, half), half)
    psend[...] = pacc[theirs, :].astype(jnp.bfloat16)
    p_cp = remote(psend, precv, s_sib.at[5], r_sib.at[5], sib)
    p_cp.start()
    my_cols = pl.multiple_of(c * GRP * HD, GRP * HD)
    for h in range(GRP):
        out[:, pl.ds(my_cols + h * HD, HD)] = result(c, h)
    p_cp.wait()
    ours = pl.ds(pl.multiple_of(c * half, half), half)
    pages[...] = (pacc[ours, :] + precv[...].astype(jnp.float32)).astype(jnp.bfloat16)
    o_cp.wait()
    out[:, pl.ds(pl.multiple_of((1 - c) * GRP * HD, GRP * HD), GRP * HD)] = orecv[...]

    for cp in sends:
        cp.wait_send()

    def ring_sent(t):
        for j in range(len(CUTS)):
            for s in range(4):
                if s % 2 == 0:
                    ring_copy(s, j, t, own.at[s // 2]).wait_send()
                else:

                    @pl.when(t < STEPS - 1)
                    def _():
                        ring_copy(s, j, t, own.at[s // 2]).wait_send()

    repeat(0, STEPS, ring_sent)


def body(tokens, block_ids, lengths, page_table, qkv_weight, q_gain, k_gain):
    own_ids = block_ids[0]
    blk_rows = ROWS // 2
    positions = (
        own_ids[:, None] * blk_rows + jnp.arange(blk_rows, dtype=jnp.int32)[None, :]
    ).reshape(ROWS)
    half = HD // 2
    channel = jnp.arange(half).astype(jnp.float32)
    inverse = jnp.power(jnp.float32(ROPE_BASE), -2.0 * channel / HD)
    pos_f = positions.astype(jnp.float32)
    angles = pos_f[:, None] * inverse[None, :]
    meta = jnp.concatenate(
        [jnp.cos(angles), jnp.sin(angles), jnp.broadcast_to(pos_f[:, None], (ROWS, ROWS))], axis=-1
    )
    ids = jnp.broadcast_to(
        jnp.repeat(own_ids, blk_rows).astype(jnp.bfloat16)[None, :], (16, ROWS)
    )
    blk = lax.axis_index("blk")
    core = blk % 2
    w = jnp.stack(
        [
            jnp.concatenate(
                [
                    qkv_weight[:, H * HD + g * HD : H * HD + (g + 1) * HD],
                    qkv_weight[:, (H + KVH + g) * HD : (H + KVH + g + 1) * HD],
                    qkv_weight[:, g * GRP * HD : (g + 1) * GRP * HD],
                ],
                axis=-1,
            )
            for g in range(KVH)
        ]
    )
    my_slots = (blk // 2) * 8 + jnp.arange(8, dtype=jnp.int32)
    table = lax.dynamic_index_in_dim(page_table[0], core, 0, keepdims=False)
    match = table[None, :] == my_slots[:, None]
    block_no = jnp.sum(
        jnp.where(match, jnp.arange(table.shape[0], dtype=jnp.int32)[None, :] + 1, 0), axis=1
    ) - 1
    wanted = block_no[:, None] * blk_rows + jnp.arange(blk_rows, dtype=jnp.int32)[None, :]
    wanted = jnp.where((block_no[:, None] >= 0) & (wanted < lengths[0]), wanted, -1)
    tpos = jnp.broadcast_to(
        wanted.reshape(8 * blk_rows, 1).astype(jnp.float32), (8 * blk_rows, ROWS)
    )

    vm = pl.BlockSpec(memory_space=pltpu.VMEM)
    dma = pltpu.SemaphoreType.DMA
    bf, f32 = jnp.bfloat16, jnp.float32
    attended, cache = pl.pallas_call(
        kernel,
        out_shape=(
            jax.ShapeDtypeStruct((ROWS, H * HD), bf),
            jax.ShapeDtypeStruct((4 * 64, 2 * HD), bf),
        ),
        in_specs=[vm] * 7 + [pl.BlockSpec(memory_space=pltpu.SMEM)],
        out_specs=(vm, vm),
        scratch_shapes=[
            pltpu.VMEM((2 * ROWS, 2048), bf),
            pltpu.VMEM((2 * ROWS, 3 * ROWS), f32),
            pltpu.VMEM((2, 16, ROWS), bf),
            pltpu.VMEM((8, 6 * HD), bf),
            pltpu.VMEM((NX, NZ, NY, 16, HD), bf),
            pltpu.VMEM((NX, NZ, NY, 16, HD), bf),
            pltpu.VMEM((NX, NZ, NY, 16, GRP * HD), bf),
            pltpu.VMEM((2, UNIT, HD), bf),
            pltpu.VMEM((4, STEPS, UNIT, HD), bf),
            pltpu.VMEM((GRP * 2 * ROWS, HD), bf),
            pltpu.VMEM((GRP * 2 * ROWS, ROWS), f32),
            pltpu.VMEM((GRP * 2 * ROWS, ROWS), f32),
            pltpu.VMEM((GRP * 2 * ROWS, HD), f32),
            pltpu.VMEM((8 * 64, 2 * HD), f32),
            pltpu.VMEM((ROWS, GRP * HD), bf),
            pltpu.VMEM((ROWS, GRP * HD), bf),
            pltpu.VMEM((4 * 64, 2 * HD), bf),
            pltpu.VMEM((4 * 64, 2 * HD), bf),
            dma((6,)),
            dma((6,)),
            dma((8, 7)),
            dma((8, 7)),
            dma((6,)),
            dma((6,)),
            dma((4, STEPS, len(CUTS))),
            dma((4, STEPS, len(CUTS))),
            dma((3,)),
        ],
        compiler_params=pltpu.CompilerParams(
            collective_id=0, has_side_effects=True, vmem_limit_bytes=56 << 20
        ),
        name="prefill",
    )(
        tokens[0],
        meta,
        ids,
        w,
        q_gain.reshape(1, HD),
        k_gain.reshape(1, HD),
        tpos,
        lengths,
    )
    return (attended[None], cache.reshape(1, 4, 64, 2 * HD))


def solution(mesh):
    in_specs = (
        P("req", "blk", None),
        P("req", "blk"),
        P("req"),
        P("req", None, None),
        P(("req", "blk"), None),
        P(),
        P(),
    )
    out_specs = (P("req", "blk", None), P("req", "blk", None, None))
    return jax.shard_map(body, mesh=mesh, in_specs=in_specs, out_specs=out_specs, check_vma=False)
```

```python
import jax
import jax.numpy as jnp
from jax import lax
from jax.experimental import pallas as pl
from jax.experimental.pallas import tpu as pltpu
from jax.sharding import PartitionSpec as P

H = 8
KVH = 2
HD = 256
GRP = H // KVH
ROPE_BASE = 1000000.0
NORM_EPS = 1e-06
FLOOR_SCORE = -1e30
MESH = pl.DeviceIdType.MESH

NX, NY, NZ = 4, 4, 8
ROWS = 128
UNIT = 2 * ROWS + 16
PIECES = ((0, ROWS + 16), (ROWS + 16, ROWS))
ORDER = ["a0", "b0", "a1", "a7", "b1", "b7", "a2", "a6", "b2", "b6", "a3", "a5", "b3", "b5", "a4", "b4"]
SLOT = {name: i for i, name in enumerate(ORDER)}

OFFS = {"x": (1, 3, 2), "y": (1, 3, 2), "z": (1, 7, 2, 6, 3, 5, 4)}
SIZE = {"x": NX, "y": NY, "z": NZ}


def kernel(
    tok, w, qg, kg, inverse, table, ids, length,
    out, pages,
    tokb, metab, idb, tpos, wout, wtmp, wk, wv, wq0, wq1, kv, qb, mb, lb, acc, pacc,
    osend, orecv, psend, precv,
    s_sib, r_sib, s_w, r_w, s_qx, r_qx, s_a, r_a, s_b, r_b, s_y, r_y, s_loc,
):
    r = lax.axis_index("req")
    b = lax.axis_index("blk")
    c = b % 2
    y = (b // 2) % NY
    z = b // (2 * NY)

    def dev(x_, y_, z_):
        return (x_, (z_ * NY + y_) * 2 + c)

    sib = (r, b + 1 - 2 * c)
    here = {"x": r, "y": y, "z": z}

    def along(ax, k):
        at = dict(here)
        at[ax] = (here[ax] + k) % SIZE[ax]
        return dev(at["x"], at["y"], at["z"])

    barrier = pltpu.get_barrier_semaphore()
    partners = [sib] + [along(ax, k) for ax in "xyz" for k in OFFS[ax]]
    for d in partners:
        pl.semaphore_signal(barrier, inc=1, device_id=d, device_id_type=MESH)
    pl.semaphore_wait(barrier, len(partners))

    def remote(src, dst, ss, rs, d):
        return pltpu.make_async_remote_copy(
            src_ref=src, dst_ref=dst, send_sem=ss, recv_sem=rs, device_id=d, device_id_type=MESH
        )

    mine = pl.ds(pl.multiple_of(c * ROWS, ROWS), ROWS)
    other = pl.ds(pl.multiple_of((1 - c) * ROWS, ROWS), ROWS)
    q_cols = GRP * HD

    def columns(core):
        at = lambda start, size: w[:, pl.ds(pl.multiple_of(start, HD), size)]
        return jnp.concatenate(
            [
                at((H + core) * HD, HD),
                at((H + KVH + core) * HD, HD),
                at(core * q_cols, q_cols),
            ],
            axis=-1,
        )

    wout[...] = columns(1 - c)
    swap = [
        (wout, wtmp, wtmp),
        (tok, tokb.at[mine], tokb.at[other]),
        (metab.at[mine], metab.at[mine], metab.at[other]),
        (idb.at[c], idb.at[c], idb.at[1 - c]),
    ]
    sends = []

    def sib_send(i):
        src, dst, _ = swap[i]
        cp = remote(src, dst, s_sib.at[i], r_sib.at[i], sib)
        cp.start()
        sends.append(cp)

    def sib_recv(i):
        src, _, arrives = swap[i]
        remote(src, arrives, s_sib.at[i], r_sib.at[i], sib).wait_recv()

    sib_send(0)
    sib_send(1)
    local = [pltpu.make_async_copy(tok, tokb.at[mine], s_loc.at[0])]
    for cp in local:
        cp.start()

    sib_recv(0)
    w_own = columns(c).astype(jnp.float32)
    w_sib = wtmp[...].astype(jnp.float32)
    first = c == 0
    rows16 = jnp.concatenate(
        [jnp.where(first, w_own, w_sib), jnp.where(first, w_sib, w_own)], axis=0
    ).astype(jnp.bfloat16)
    wk[r, z, y] = rows16[:, :HD]
    wv[r, z, y] = rows16[:, HD : 2 * HD]
    wq0[r, z, y] = rows16[:, 2 * HD : 4 * HD]
    wq1[r, z, y] = rows16[:, 4 * HD :]

    def region(done, at):
        return tuple(slice(None) if ax in done else at[ax] for ax in "xzy")

    def phase(number, wb, done, ax):
        pairs = []
        for k, off in enumerate(OFFS[ax]):
            came = dict(here)
            came[ax] = (here[ax] - off + SIZE[ax]) % SIZE[ax]
            src = wb.at[region(done, here)]
            ss, rs, d = s_w.at[number, k], r_w.at[number, k], along(ax, off)
            pairs.append(
                (remote(src, src, ss, rs, d), remote(src, wb.at[region(done, came)], ss, rs, d))
            )
        for cp, _ in pairs:
            cp.start()
            sends.append(cp)
        return [arrive for _, arrive in pairs]

    def arrived(copies):
        for cp in copies:
            cp.wait_recv()

    k1 = phase(0, wk, "", "z")
    v1 = phase(1, wv, "", "z")
    q01 = phase(2, wq0, "", "y")
    q11 = phase(3, wq1, "", "y")
    arrived(k1)
    k2 = phase(4, wk, "z", "y")
    arrived(v1)
    v2 = phase(5, wv, "z", "x")
    arrived(q01)
    q02 = phase(6, wq0, "y", "z")
    arrived(k2)
    k3 = phase(7, wk, "zy", "x")
    arrived(v2)
    v3 = phase(8, wv, "zx", "y")
    arrived(q11)
    q12 = phase(9, wq1, "y", "z")

    blk_rows = ROWS // 2
    row = lax.broadcasted_iota(jnp.int32, (ROWS, ROWS), 0)
    lane_no = lax.broadcasted_iota(jnp.int32, (16, ROWS), 1)
    pos = jnp.where(row < blk_rows, ids[0], ids[1]) * blk_rows + row % blk_rows
    pos_f = pos.astype(jnp.float32)
    angles = pos_f * inverse[...]
    metab[mine, :ROWS] = jnp.cos(angles)
    metab[mine, ROWS : 2 * ROWS] = jnp.sin(angles)
    metab[mine, 2 * ROWS :] = pos_f
    numbers = jnp.where(lane_no < blk_rows, ids[0], ids[1])
    idb[c] = numbers.astype(jnp.float32).astype(jnp.bfloat16)
    sib_send(2)
    sib_send(3)

    entries = table[pl.ds(c, 1), :]
    block_of = lax.broadcasted_iota(jnp.int32, (1, ROWS), 1).astype(jnp.float32)
    row_f = lax.broadcasted_iota(jnp.int32, (blk_rows, ROWS), 0).astype(jnp.float32)
    for i in range(8):
        slot = (b // 2) * 8 + i
        found = jnp.max(jnp.where(entries == slot, block_of, -1.0), axis=-1, keepdims=True)
        wanted = found * blk_rows + row_f
        keep = (found >= 0.0) & (wanted < length[0].astype(jnp.float32))
        tpos[i * blk_rows : (i + 1) * blk_rows, :] = jnp.where(keep, wanted, -1.0)

    mb[...] = jnp.full_like(mb, FLOOR_SCORE)
    lb[...] = jnp.zeros_like(lb)
    acc[...] = jnp.zeros_like(acc)
    pacc[...] = jnp.zeros_like(pacc)
    for i in (1, 2, 3):
        sib_recv(i)
    for cp in local:
        cp.wait()

    def normed(u, gain):
        scaled = u * lax.rsqrt(jnp.mean(u * u, axis=-1, keepdims=True) + NORM_EPS)
        return scaled if gain is None else scaled * gain[...]

    def rotated(u):
        half = HD // 2
        cosine = metab[:, :half]
        sine = metab[:, half : 2 * half]
        front, second = u[:, :half], u[:, half:]
        return jnp.concatenate(
            [front * cosine - second * sine, second * cosine + front * sine], axis=-1
        )

    def project(weights):
        return jnp.dot(
            tokb[...],
            weights.reshape(NX * NY * NZ * 16, HD),
            preferred_element_type=jnp.float32,
        )

    halves = (pl.ds(0, NZ // 2), pl.ds(NZ // 2, NZ // 2))
    nxt, prv = along("x", 1), along("x", NX - 1)
    x_prv, x_nxt, x_far = (r + NX - 1) % NX, (r + 1) % NX, (r + 2) % NX

    def q_copy(part, n, plane, half, d):
        ref = (wq0, wq1)[part].at[plane, halves[half]]
        return remote(ref, ref, s_qx.at[part, n], r_qx.at[part, n], d)

    def begin(copies):
        for cp in copies:
            cp.start()
            sends.append(cp)

    def q_hop1(p):
        begin(
            [
                q_copy(p, 0, r, 0, nxt),
                q_copy(p, 1, r, 1, prv),
                q_copy(p, 2, r, 1, nxt),
                q_copy(p, 3, r, 0, prv),
            ]
        )

    def q_hop2(p):
        arrived([q_copy(p, 0, x_prv, 0, nxt), q_copy(p, 1, x_nxt, 1, prv)])
        begin([q_copy(p, 4, x_prv, 0, nxt), q_copy(p, 5, x_nxt, 1, prv)])

    def q_done(p):
        arrived(
            [
                q_copy(p, 2, x_prv, 1, nxt),
                q_copy(p, 3, x_nxt, 0, prv),
                q_copy(p, 4, x_far, 0, nxt),
                q_copy(p, 5, x_far, 1, prv),
            ]
        )

    def project_half(p):
        for i in range(2):
            rows = pl.ds((2 * p + i) * 2 * ROWS, 2 * ROWS)
            weights = (wq0, wq1)[p][:, :, :, :, i * HD : (i + 1) * HD]
            qb[rows, :] = rotated(normed(project(weights), qg)).astype(jnp.bfloat16)

    arrived(k3)
    arrived(q02)
    q_hop1(0)
    keys = rotated(normed(project(wk[...]), kg)).astype(jnp.bfloat16)
    own = [kv.at[SLOT["a0"], 0], kv.at[SLOT["b0"], 0]]
    for i in range(2):
        own[i][:ROWS] = keys[i * ROWS : (i + 1) * ROWS]
        own[i][ROWS : ROWS + 16] = jnp.concatenate([idb[i], idb[i]], axis=-1)
    arrived(v3)
    values = normed(project(wv[...]), None).astype(jnp.bfloat16)
    for i in range(2):
        own[i][ROWS + 16 :] = values[i * ROWS : (i + 1) * ROWS]

    to_z = (along("z", 1), along("z", NZ - 1))

    def at(kind, planes, lane):
        return kv.at[SLOT[kind + str(planes % NZ)], lane]

    def planes_after(way, hops):
        return (NZ - hops) % NZ if way == 0 else hops

    def a_copy(way, hop, lane):
        src = at("a", planes_after(way, hop - 1), lane)
        dst = at("a", planes_after(way, hop), lane)
        sem = (way, hop - 1, lane)
        return remote(src, dst, s_a.at[sem], r_a.at[sem], to_z[way])

    def b_copy(way, hop):
        src = at("b", planes_after(way, hop - 1), 0)
        dst = at("b", planes_after(way, hop), 0)
        if hop == NZ // 2:
            piece = pl.ds(*PIECES[way])
            src, dst = src.at[piece], dst.at[piece]
        return remote(src, dst, s_b.at[way, hop - 1], r_b.at[way, hop - 1], to_z[way])

    def y_copy(kind, planes, k):
        row = NZ if kind == "a" else planes % NZ
        off = OFFS["y"][k]
        return remote(
            at(kind, planes, 0),
            at(kind, planes, NY - off),
            s_y.at[row, k],
            r_y.at[row, k],
            along("y", off),
        )

    def a_ways(hop, lane):
        if hop < NZ // 2:
            return (0, 1)
        return (0,) if lane < NY // 2 else (1,)

    def a_send(hop, lane):
        begin([a_copy(way, hop, lane) for way in a_ways(hop, lane)])

    def a_arrive(hop, forward):
        for lane in range(NY):
            for way in a_ways(hop, lane):
                a_copy(way, hop, lane).wait_recv()
            if forward:
                for way in a_ways(hop + 1, lane):
                    begin([a_copy(way, hop + 1, lane)])

    def y_send(kind, planes):
        begin([y_copy(kind, planes, k) for k in range(NY - 1)])

    def y_arrive(kind, planes):
        arrived([y_copy(kind, planes, k) for k in range(NY - 1)])

    def b_arrive(hop):
        for way in range(2):
            b_copy(way, hop).wait_recv()
            if hop < NZ // 2:
                begin([b_copy(way, hop + 1)])
                y_send("b", planes_after(way, hop))
        if hop == NZ // 2:
            y_send("b", hop)

    begin([b_copy(way, 1) for way in range(2)])
    y_send("a", 0)
    a_send(1, 0)
    y_send("b", 0)

    def repeat(lo, hi, f):
        def go(t, carry):
            f(t)
            return carry

        lax.fori_loop(lo, hi, go, 0)

    limit = length[0].astype(jnp.float32)
    lane = lax.broadcasted_iota(jnp.int32, (1, ROWS), 1)
    lane_in_block = (lane % (ROWS // 2)).astype(jnp.float32)

    def attend(group, pair):
        units = [kv[group, i] for i in range(NY)]
        key_pos = []
        for u in units:
            number = u[ROWS : ROWS + 16, :ROWS].astype(jnp.float32)[:1]
            key_pos.append(number * (ROWS // 2) + lane_in_block)
        seen = [jnp.where(kp < limit, kp, 1e9) for kp in key_pos]
        keys = jnp.concatenate([u[:ROWS] for u in units], axis=0)
        values = jnp.concatenate([u[ROWS + 16 :] for u in units], axis=0)

        def head(h):
            rows = pl.ds(pl.multiple_of((2 * pair + h) * 2 * ROWS, 2 * ROWS), 2 * ROWS)
            query_pos = metab[:, HD : HD + ROWS]
            scores = lax.dot_general(
                qb[rows, :], keys, (((1,), (1,)), ((), ())), preferred_element_type=jnp.float32
            )
            parts = [
                jnp.where(sn <= query_pos, scores[:, i * ROWS : (i + 1) * ROWS], FLOOR_SCORE)
                for i, sn in enumerate(seen)
            ]
            old_max = mb[rows, :]
            top = parts[0]
            for part in parts[1:]:
                top = jnp.maximum(top, part)
            new_max = jnp.maximum(old_max, jnp.max(top, axis=-1, keepdims=True))
            rescale = jnp.exp(old_max - new_max)
            weights = [jnp.exp(part - new_max) for part in parts]
            total = weights[0]
            for wt in weights[1:]:
                total = total + wt
            mb[rows, :] = new_max
            lb[rows, :] = lb[rows, :] * rescale + total
            product = jnp.dot(
                jnp.concatenate([wt.astype(jnp.bfloat16) for wt in weights], axis=-1),
                values,
                preferred_element_type=jnp.float32,
            )
            acc[rows, :] = acc[rows, :] * jnp.concatenate([rescale, rescale], axis=-1) + product

        for h in range(2):
            head(h)

        def page_part(i):
            rows = pl.ds(pl.multiple_of(i * 2 * ROWS, 2 * ROWS), 2 * ROWS)
            wanted = tpos[rows, :]
            chosen = jnp.concatenate(
                [jnp.where(wanted == kp, 1.0, 0.0).astype(jnp.bfloat16) for kp in key_pos], axis=-1
            )
            pacc[rows, :HD] += jnp.dot(chosen, keys, preferred_element_type=jnp.float32)
            pacc[rows, HD:] += jnp.dot(chosen, values, preferred_element_type=jnp.float32)

        page_part(pair)

    def attend_groups(lo, hi, pair):
        repeat(lo, hi, lambda g: attend(g, pair))

    y_arrive("a", 0)
    for lane in range(1, NY):
        a_send(1, lane)
    b_arrive(1)
    q_hop2(0)
    arrived(q12)
    q_hop1(1)
    a_arrive(1, True)
    q_done(0)
    project_half(0)
    y_arrive("b", 0)
    attend_groups(0, 4, 0)
    b_arrive(2)
    q_hop2(1)
    for planes in (1, 7):
        y_arrive("b", planes)
    attend_groups(4, 6, 0)
    a_arrive(2, True)
    attend_groups(6, 8, 0)
    b_arrive(3)
    q_done(1)
    project_half(1)
    attend_groups(0, 6, 1)
    for planes in (2, 6):
        y_arrive("b", planes)
    attend_groups(8, 10, 0)
    a_arrive(3, True)
    b_arrive(4)
    attend_groups(10, 12, 0)
    attend_groups(6, 12, 1)
    for planes in (3, 5):
        y_arrive("b", planes)
    repeat(0, 4, lambda i: attend(12 + i // 2, i % 2))
    a_arrive(4, False)
    y_arrive("b", 4)
    repeat(0, 4, lambda i: attend(14 + i // 2, i % 2))

    def result(part, h):
        start = h * 2 * ROWS + part * ROWS
        rows = pl.ds(pl.multiple_of(start, ROWS), ROWS)
        live = metab[pl.ds(pl.multiple_of(part * ROWS, ROWS), ROWS), HD : HD + 1] < limit
        total = jnp.sum(lb[rows, :], axis=-1, keepdims=True)
        divided = acc[rows, :] / jnp.where(live, total, 1.0)
        return jnp.where(live, divided, 0.0).astype(jnp.bfloat16)

    for h in range(GRP):
        osend[:, h * HD : (h + 1) * HD] = result(1 - c, h)
    o_cp = remote(osend, orecv, s_sib.at[4], r_sib.at[4], sib)
    o_cp.start()
    half = 4 * 64
    theirs = pl.ds(pl.multiple_of((1 - c) * half, half), half)
    psend[...] = pacc[theirs, :].astype(jnp.bfloat16)
    p_cp = remote(psend, precv, s_sib.at[5], r_sib.at[5], sib)
    p_cp.start()
    my_cols = pl.multiple_of(c * GRP * HD, GRP * HD)
    for h in range(GRP):
        out[:, pl.ds(my_cols + h * HD, HD)] = result(c, h)
    p_cp.wait()
    ours = pl.ds(pl.multiple_of(c * half, half), half)
    pages[...] = (pacc[ours, :] + precv[...].astype(jnp.float32)).astype(jnp.bfloat16)
    o_cp.wait()
    out[:, pl.ds(pl.multiple_of((1 - c) * GRP * HD, GRP * HD), GRP * HD)] = orecv[...]

    for cp in sends:
        cp.wait_send()


def body(tokens, block_ids, lengths, page_table, qkv_weight, q_gain, k_gain):
    half = HD // 2
    channel = jnp.arange(half).astype(jnp.float32)
    inverse = jnp.power(jnp.float32(ROPE_BASE), -2.0 * channel / HD)
    vm = pl.BlockSpec(memory_space=pltpu.VMEM)
    dma = pltpu.SemaphoreType.DMA
    bf, f32 = jnp.bfloat16, jnp.float32
    attended, cache = pl.pallas_call(
        kernel,
        out_shape=(
            jax.ShapeDtypeStruct((ROWS, H * HD), bf),
            jax.ShapeDtypeStruct((4 * 64, 2 * HD), bf),
        ),
        in_specs=[vm] * 6 + [pl.BlockSpec(memory_space=pltpu.SMEM)] * 2,
        out_specs=(vm, vm),
        scratch_shapes=[
            pltpu.VMEM((2 * ROWS, 2048), bf),
            pltpu.VMEM((2 * ROWS, 3 * ROWS), f32),
            pltpu.VMEM((2, 16, ROWS), bf),
            pltpu.VMEM((8 * 64, ROWS), f32),
            pltpu.VMEM((8, 6 * HD), bf),
            pltpu.VMEM((8, 6 * HD), bf),
            pltpu.VMEM((NX, NZ, NY, 16, HD), bf),
            pltpu.VMEM((NX, NZ, NY, 16, HD), bf),
            pltpu.VMEM((NX, NZ, NY, 16, 2 * HD), bf),
            pltpu.VMEM((NX, NZ, NY, 16, 2 * HD), bf),
            pltpu.VMEM((2 * NZ, NY, UNIT, HD), bf),
            pltpu.VMEM((GRP * 2 * ROWS, HD), bf),
            pltpu.VMEM((GRP * 2 * ROWS, ROWS), f32),
            pltpu.VMEM((GRP * 2 * ROWS, ROWS), f32),
            pltpu.VMEM((GRP * 2 * ROWS, HD), f32),
            pltpu.VMEM((8 * 64, 2 * HD), f32),
            pltpu.VMEM((ROWS, GRP * HD), bf),
            pltpu.VMEM((ROWS, GRP * HD), bf),
            pltpu.VMEM((4 * 64, 2 * HD), bf),
            pltpu.VMEM((4 * 64, 2 * HD), bf),
            dma((6,)),
            dma((6,)),
            dma((10, 7)),
            dma((10, 7)),
            dma((2, 6)),
            dma((2, 6)),
            dma((2, NZ // 2, NY)),
            dma((2, NZ // 2, NY)),
            dma((2, NZ // 2)),
            dma((2, NZ // 2)),
            dma((NZ + 1, NY - 1)),
            dma((NZ + 1, NY - 1)),
            dma((1,)),
        ],
        compiler_params=pltpu.CompilerParams(
            collective_id=0, has_side_effects=True, vmem_limit_bytes=56 << 20
        ),
        name="prefill",
    )(
        tokens[0],
        qkv_weight,
        q_gain.reshape(1, HD),
        k_gain.reshape(1, HD),
        inverse.reshape(1, half),
        page_table[0],
        block_ids[0],
        lengths,
    )
    return (attended[None], cache.reshape(1, 4, 64, 2 * HD))


def solution(mesh):
    in_specs = (
        P("req", "blk", None),
        P("req", "blk"),
        P("req"),
        P("req", None, None),
        P(("req", "blk"), None),
        P(),
        P(),
    )
    out_specs = (P("req", "blk", None), P("req", "blk", None, None))
    return jax.shard_map(body, mesh=mesh, in_specs=in_specs, out_specs=out_specs, check_vma=False)
```

```python
import jax
import jax.numpy as jnp
from jax import lax
from jax.experimental import pallas as pl
from jax.experimental.pallas import tpu as pltpu
from jax.sharding import PartitionSpec as P

H = 8
KVH = 2
HD = 256
GRP = H // KVH
ROPE_BASE = 1000000.0
NORM_EPS = 1e-06
FLOOR_SCORE = -1e30
MESH = pl.DeviceIdType.MESH

NX, NY, NZ = 4, 4, 8
ROWS = 128
UNIT = 2 * ROWS + 16
PIECES = ((0, ROWS + 16), (ROWS + 16, ROWS))
ORDER = ["a0", "b0", "a1", "a7", "b1", "b7", "a2", "a6", "b2", "b6", "a3", "a5", "b3", "b5", "a4", "b4"]
SLOT = {name: i for i, name in enumerate(ORDER)}

OFFS = {"x": (1, 3, 2), "y": (1, 3, 2), "z": (1, 7, 2, 6, 3, 5, 4)}
SIZE = {"x": NX, "y": NY, "z": NZ}


def kernel(
    tok, w, qg, kg, inverse, table, ids, length,
    out, pages,
    tokb, metab, idb, tpos, wout, wtmp, wk, wv, wq0, wq1, kv, qb, mb, lb, acc, pacc,
    osend, orecv, psend, precv,
    s_sib, r_sib, s_w, r_w, s_qx, r_qx, s_a, r_a, s_b, r_b, s_y, r_y, s_loc,
):
    r = lax.axis_index("req")
    b = lax.axis_index("blk")
    c = b % 2
    y = (b // 2) % NY
    z = b // (2 * NY)

    def dev(x_, y_, z_):
        return (x_, (z_ * NY + y_) * 2 + c)

    sib = (r, b + 1 - 2 * c)
    here = {"x": r, "y": y, "z": z}

    def along(ax, k):
        at = dict(here)
        at[ax] = (here[ax] + k) % SIZE[ax]
        return dev(at["x"], at["y"], at["z"])

    barrier = pltpu.get_barrier_semaphore()
    partners = [sib] + [along(ax, k) for ax in "xyz" for k in OFFS[ax]]
    for d in partners:
        pl.semaphore_signal(barrier, inc=1, device_id=d, device_id_type=MESH)
    pl.semaphore_wait(barrier, len(partners))

    def remote(src, dst, ss, rs, d):
        return pltpu.make_async_remote_copy(
            src_ref=src, dst_ref=dst, send_sem=ss, recv_sem=rs, device_id=d, device_id_type=MESH
        )

    mine = pl.ds(pl.multiple_of(c * ROWS, ROWS), ROWS)
    other = pl.ds(pl.multiple_of((1 - c) * ROWS, ROWS), ROWS)
    q_cols = GRP * HD

    def columns(core):
        at = lambda start, size: w[:, pl.ds(pl.multiple_of(start, HD), size)]
        return jnp.concatenate(
            [
                at((H + core) * HD, HD),
                at((H + KVH + core) * HD, HD),
                at(core * q_cols, q_cols),
            ],
            axis=-1,
        )

    wout[...] = columns(1 - c)
    swap = [
        (wout, wtmp, wtmp),
        (tok, tokb.at[mine], tokb.at[other]),
        (metab.at[mine], metab.at[mine], metab.at[other]),
        (idb.at[c], idb.at[c], idb.at[1 - c]),
    ]
    sends = []

    def sib_send(i):
        src, dst, _ = swap[i]
        cp = remote(src, dst, s_sib.at[i], r_sib.at[i], sib)
        cp.start()
        sends.append(cp)

    def sib_recv(i):
        src, _, arrives = swap[i]
        remote(src, arrives, s_sib.at[i], r_sib.at[i], sib).wait_recv()

    sib_send(0)
    sib_send(1)
    local = [pltpu.make_async_copy(tok, tokb.at[mine], s_loc.at[0])]
    for cp in local:
        cp.start()

    sib_recv(0)
    w_own = columns(c).astype(jnp.float32)
    w_sib = wtmp[...].astype(jnp.float32)
    first = c == 0
    rows16 = jnp.concatenate(
        [jnp.where(first, w_own, w_sib), jnp.where(first, w_sib, w_own)], axis=0
    ).astype(jnp.bfloat16)
    wk[r, z, y] = rows16[:, :HD]
    wv[r, z, y] = rows16[:, HD : 2 * HD]
    wq0[r, z, y] = rows16[:, 2 * HD : 4 * HD]
    wq1[r, z, y] = rows16[:, 4 * HD :]

    def region(done, at):
        return tuple(slice(None) if ax in done else at[ax] for ax in "xzy")

    def phase(number, wb, done, ax):
        pairs = []
        for k, off in enumerate(OFFS[ax]):
            came = dict(here)
            came[ax] = (here[ax] - off + SIZE[ax]) % SIZE[ax]
            src = wb.at[region(done, here)]
            ss, rs, d = s_w.at[number, k], r_w.at[number, k], along(ax, off)
            pairs.append(
                (remote(src, src, ss, rs, d), remote(src, wb.at[region(done, came)], ss, rs, d))
            )
        for cp, _ in pairs:
            cp.start()
            sends.append(cp)
        return [arrive for _, arrive in pairs]

    def arrived(copies):
        for cp in copies:
            cp.wait_recv()

    k1 = phase(0, wk, "", "z")
    v1 = phase(1, wv, "", "z")
    q01 = phase(2, wq0, "", "y")
    q11 = phase(3, wq1, "", "y")
    arrived(k1)
    k2 = phase(4, wk, "z", "y")
    arrived(v1)
    v2 = phase(5, wv, "z", "x")
    arrived(q01)
    q02 = phase(6, wq0, "y", "z")
    arrived(k2)
    k3 = phase(7, wk, "zy", "x")
    arrived(v2)
    v3 = phase(8, wv, "zx", "y")
    arrived(q11)
    q12 = phase(9, wq1, "y", "z")

    blk_rows = ROWS // 2
    row = lax.broadcasted_iota(jnp.int32, (ROWS, ROWS), 0)
    lane_no = lax.broadcasted_iota(jnp.int32, (16, ROWS), 1)
    pos = jnp.where(row < blk_rows, ids[0], ids[1]) * blk_rows + row % blk_rows
    pos_f = pos.astype(jnp.float32)
    angles = pos_f * inverse[...]
    metab[mine, :ROWS] = jnp.cos(angles)
    metab[mine, ROWS : 2 * ROWS] = jnp.sin(angles)
    metab[mine, 2 * ROWS :] = pos_f
    numbers = jnp.where(lane_no < blk_rows, ids[0], ids[1])
    idb[c] = numbers.astype(jnp.float32).astype(jnp.bfloat16)
    sib_send(2)
    sib_send(3)

    entries = table[pl.ds(c, 1), :]
    block_of = lax.broadcasted_iota(jnp.int32, (1, ROWS), 1).astype(jnp.float32)
    row_f = lax.broadcasted_iota(jnp.int32, (blk_rows, ROWS), 0).astype(jnp.float32)
    for i in range(8):
        slot = (b // 2) * 8 + i
        found = jnp.max(jnp.where(entries == slot, block_of, -1.0), axis=-1, keepdims=True)
        wanted = found * blk_rows + row_f
        keep = (found >= 0.0) & (wanted < length[0].astype(jnp.float32))
        tpos[i * blk_rows : (i + 1) * blk_rows, :] = jnp.where(keep, wanted, -1.0)

    mb[...] = jnp.full_like(mb, FLOOR_SCORE)
    lb[...] = jnp.zeros_like(lb)
    acc[...] = jnp.zeros_like(acc)
    pacc[...] = jnp.zeros_like(pacc)
    for i in (1, 2, 3):
        sib_recv(i)
    for cp in local:
        cp.wait()

    def normed(u, gain):
        scaled = u * lax.rsqrt(jnp.mean(u * u, axis=-1, keepdims=True) + NORM_EPS)
        return scaled if gain is None else scaled * gain[...]

    def rotated(u):
        half = HD // 2
        cosine = metab[:, :half]
        sine = metab[:, half : 2 * half]
        front, second = u[:, :half], u[:, half:]
        return jnp.concatenate(
            [front * cosine - second * sine, second * cosine + front * sine], axis=-1
        )

    def project(weights):
        return jnp.dot(
            tokb[...],
            weights.reshape(NX * NY * NZ * 16, HD),
            preferred_element_type=jnp.float32,
        )

    halves = (pl.ds(0, NZ // 2), pl.ds(NZ // 2, NZ // 2))
    nxt, prv = along("x", 1), along("x", NX - 1)
    x_prv, x_nxt, x_far = (r + NX - 1) % NX, (r + 1) % NX, (r + 2) % NX

    def q_copy(part, n, plane, half, d):
        ref = (wq0, wq1)[part].at[plane, halves[half]]
        return remote(ref, ref, s_qx.at[part, n], r_qx.at[part, n], d)

    def begin(copies):
        for cp in copies:
            cp.start()
            sends.append(cp)

    def q_hop1(p):
        begin(
            [
                q_copy(p, 0, r, 0, nxt),
                q_copy(p, 1, r, 1, prv),
                q_copy(p, 2, r, 1, nxt),
                q_copy(p, 3, r, 0, prv),
            ]
        )

    def q_hop2(p):
        arrived([q_copy(p, 0, x_prv, 0, nxt), q_copy(p, 1, x_nxt, 1, prv)])
        begin([q_copy(p, 4, x_prv, 0, nxt), q_copy(p, 5, x_nxt, 1, prv)])

    def q_done(p):
        arrived(
            [
                q_copy(p, 2, x_prv, 1, nxt),
                q_copy(p, 3, x_nxt, 0, prv),
                q_copy(p, 4, x_far, 0, nxt),
                q_copy(p, 5, x_far, 1, prv),
            ]
        )

    def project_half(p):
        for i in range(2):
            rows = pl.ds((2 * p + i) * 2 * ROWS, 2 * ROWS)
            weights = (wq0, wq1)[p][:, :, :, :, i * HD : (i + 1) * HD]
            qb[rows, :] = rotated(normed(project(weights), qg)).astype(jnp.bfloat16)

    arrived(k3)
    arrived(q02)
    q_hop1(0)
    keys = rotated(normed(project(wk[...]), kg)).astype(jnp.bfloat16)
    own = [kv.at[SLOT["a0"], 0], kv.at[SLOT["b0"], 0]]
    for i in range(2):
        own[i][:ROWS] = keys[i * ROWS : (i + 1) * ROWS]
        own[i][ROWS : ROWS + 16] = jnp.concatenate([idb[i], idb[i]], axis=-1)
    arrived(v3)
    values = normed(project(wv[...]), None).astype(jnp.bfloat16)
    for i in range(2):
        own[i][ROWS + 16 :] = values[i * ROWS : (i + 1) * ROWS]

    to_z = (along("z", 1), along("z", NZ - 1))

    def at(kind, planes, lane):
        return kv.at[SLOT[kind + str(planes % NZ)], lane]

    def planes_after(way, hops):
        return (NZ - hops) % NZ if way == 0 else hops

    def a_copy(way, hop, lane):
        src = at("a", planes_after(way, hop - 1), lane)
        dst = at("a", planes_after(way, hop), lane)
        sem = (way, hop - 1, lane)
        return remote(src, dst, s_a.at[sem], r_a.at[sem], to_z[way])

    def b_copy(way, hop):
        src = at("b", planes_after(way, hop - 1), 0)
        dst = at("b", planes_after(way, hop), 0)
        if hop == NZ // 2:
            piece = pl.ds(*PIECES[way])
            src, dst = src.at[piece], dst.at[piece]
        return remote(src, dst, s_b.at[way, hop - 1], r_b.at[way, hop - 1], to_z[way])

    def y_copy(kind, planes, k):
        row = NZ if kind == "a" else planes % NZ
        off = OFFS["y"][k]
        return remote(
            at(kind, planes, 0),
            at(kind, planes, NY - off),
            s_y.at[row, k],
            r_y.at[row, k],
            along("y", off),
        )

    def a_ways(hop, lane):
        if hop < NZ // 2:
            return (0, 1)
        return (0,) if lane < NY // 2 else (1,)

    def a_send(hop, lane):
        begin([a_copy(way, hop, lane) for way in a_ways(hop, lane)])

    def a_arrive(hop, forward):
        for lane in range(NY):
            for way in a_ways(hop, lane):
                a_copy(way, hop, lane).wait_recv()
            if forward:
                for way in a_ways(hop + 1, lane):
                    begin([a_copy(way, hop + 1, lane)])

    def y_send(kind, planes):
        begin([y_copy(kind, planes, k) for k in range(NY - 1)])

    def y_arrive(kind, planes):
        arrived([y_copy(kind, planes, k) for k in range(NY - 1)])

    def b_arrive(hop):
        for way in range(2):
            b_copy(way, hop).wait_recv()
            if hop < NZ // 2:
                begin([b_copy(way, hop + 1)])
                y_send("b", planes_after(way, hop))
        if hop == NZ // 2:
            y_send("b", hop)

    begin([b_copy(way, 1) for way in range(2)])
    y_send("a", 0)
    a_send(1, 0)
    y_send("b", 0)

    def repeat(lo, hi, f):
        def go(t, carry):
            f(t)
            return carry

        lax.fori_loop(lo, hi, go, 0)

    limit = length[0].astype(jnp.float32)
    lane = lax.broadcasted_iota(jnp.int32, (1, ROWS), 1)
    lane_in_block = (lane % (ROWS // 2)).astype(jnp.float32)

    def attend(group, pair):
        units = [kv[group, i] for i in range(NY)]
        key_pos = []
        for u in units:
            number = u[ROWS : ROWS + 16, :ROWS].astype(jnp.float32)[:1]
            key_pos.append(number * (ROWS // 2) + lane_in_block)
        seen = [jnp.where(kp < limit, kp, 1e9) for kp in key_pos]
        keys = jnp.concatenate([u[:ROWS] for u in units], axis=0)
        values = jnp.concatenate([u[ROWS + 16 :] for u in units], axis=0)

        def head(h):
            rows = pl.ds(pl.multiple_of((2 * pair + h) * 2 * ROWS, 2 * ROWS), 2 * ROWS)
            query_pos = metab[:, HD : HD + ROWS]
            scores = lax.dot_general(
                qb[rows, :], keys, (((1,), (1,)), ((), ())), preferred_element_type=jnp.float32
            )
            parts = [
                jnp.where(sn <= query_pos, scores[:, i * ROWS : (i + 1) * ROWS], FLOOR_SCORE)
                for i, sn in enumerate(seen)
            ]
            old_max = mb[rows, :]
            top = parts[0]
            for part in parts[1:]:
                top = jnp.maximum(top, part)
            new_max = jnp.maximum(old_max, jnp.max(top, axis=-1, keepdims=True))
            rescale = jnp.exp(old_max - new_max)
            weights = [jnp.exp(part - new_max) for part in parts]
            total = weights[0]
            for wt in weights[1:]:
                total = total + wt
            mb[rows, :] = new_max
            lb[rows, :] = lb[rows, :] * rescale + total
            product = jnp.dot(
                jnp.concatenate([wt.astype(jnp.bfloat16) for wt in weights], axis=-1),
                values,
                preferred_element_type=jnp.float32,
            )
            acc[rows, :] = acc[rows, :] * jnp.concatenate([rescale, rescale], axis=-1) + product

        for h in range(2):
            head(h)

        def page_part(i):
            rows = pl.ds(pl.multiple_of(i * 2 * ROWS, 2 * ROWS), 2 * ROWS)
            wanted = tpos[rows, :]
            chosen = jnp.concatenate(
                [jnp.where(wanted == kp, 1.0, 0.0).astype(jnp.bfloat16) for kp in key_pos], axis=-1
            )
            pacc[rows, :HD] += jnp.dot(chosen, keys, preferred_element_type=jnp.float32)
            pacc[rows, HD:] += jnp.dot(chosen, values, preferred_element_type=jnp.float32)

        page_part(pair)

    def attend_groups(lo, hi, pair):
        repeat(lo, hi, lambda g: attend(g, pair))

    y_arrive("a", 0)
    for lane in range(1, NY):
        a_send(1, lane)
    b_arrive(1)
    q_hop2(0)
    arrived(q12)
    q_hop1(1)
    a_arrive(1, True)
    q_done(0)
    project_half(0)
    y_arrive("b", 0)
    attend_groups(0, 4, 0)
    b_arrive(2)
    q_hop2(1)
    for planes in (1, 7):
        y_arrive("b", planes)
    attend_groups(4, 6, 0)
    a_arrive(2, True)
    attend_groups(6, 8, 0)
    b_arrive(3)
    q_done(1)
    project_half(1)
    attend_groups(0, 6, 1)
    for planes in (2, 6):
        y_arrive("b", planes)
    attend_groups(8, 10, 0)
    a_arrive(3, True)
    attend_groups(10, 12, 0)
    attend_groups(6, 9, 1)
    b_arrive(4)
    attend_groups(9, 12, 1)
    for planes in (3, 5):
        y_arrive("b", planes)
    repeat(0, 4, lambda i: attend(12 + i // 2, i % 2))
    a_arrive(4, False)
    y_arrive("b", 4)
    repeat(0, 4, lambda i: attend(14 + i // 2, i % 2))

    def result(part, h):
        start = h * 2 * ROWS + part * ROWS
        rows = pl.ds(pl.multiple_of(start, ROWS), ROWS)
        live = metab[pl.ds(pl.multiple_of(part * ROWS, ROWS), ROWS), HD : HD + 1] < limit
        total = jnp.sum(lb[rows, :], axis=-1, keepdims=True)
        divided = acc[rows, :] / jnp.where(live, total, 1.0)
        return jnp.where(live, divided, 0.0).astype(jnp.bfloat16)

    for h in range(GRP):
        osend[:, h * HD : (h + 1) * HD] = result(1 - c, h)
    o_cp = remote(osend, orecv, s_sib.at[4], r_sib.at[4], sib)
    o_cp.start()
    half = 4 * 64
    theirs = pl.ds(pl.multiple_of((1 - c) * half, half), half)
    psend[...] = pacc[theirs, :].astype(jnp.bfloat16)
    p_cp = remote(psend, precv, s_sib.at[5], r_sib.at[5], sib)
    p_cp.start()
    my_cols = pl.multiple_of(c * GRP * HD, GRP * HD)
    for h in range(GRP):
        out[:, pl.ds(my_cols + h * HD, HD)] = result(c, h)
    p_cp.wait()
    ours = pl.ds(pl.multiple_of(c * half, half), half)
    pages[...] = (pacc[ours, :] + precv[...].astype(jnp.float32)).astype(jnp.bfloat16)
    o_cp.wait()
    out[:, pl.ds(pl.multiple_of((1 - c) * GRP * HD, GRP * HD), GRP * HD)] = orecv[...]

    for cp in sends:
        cp.wait_send()


def body(tokens, block_ids, lengths, page_table, qkv_weight, q_gain, k_gain):
    half = HD // 2
    channel = jnp.arange(half).astype(jnp.float32)
    inverse = jnp.power(jnp.float32(ROPE_BASE), -2.0 * channel / HD)
    vm = pl.BlockSpec(memory_space=pltpu.VMEM)
    dma = pltpu.SemaphoreType.DMA
    bf, f32 = jnp.bfloat16, jnp.float32
    attended, cache = pl.pallas_call(
        kernel,
        out_shape=(
            jax.ShapeDtypeStruct((ROWS, H * HD), bf),
            jax.ShapeDtypeStruct((4 * 64, 2 * HD), bf),
        ),
        in_specs=[vm] * 6 + [pl.BlockSpec(memory_space=pltpu.SMEM)] * 2,
        out_specs=(vm, vm),
        scratch_shapes=[
            pltpu.VMEM((2 * ROWS, 2048), bf),
            pltpu.VMEM((2 * ROWS, 3 * ROWS), f32),
            pltpu.VMEM((2, 16, ROWS), bf),
            pltpu.VMEM((8 * 64, ROWS), f32),
            pltpu.VMEM((8, 6 * HD), bf),
            pltpu.VMEM((8, 6 * HD), bf),
            pltpu.VMEM((NX, NZ, NY, 16, HD), bf),
            pltpu.VMEM((NX, NZ, NY, 16, HD), bf),
            pltpu.VMEM((NX, NZ, NY, 16, 2 * HD), bf),
            pltpu.VMEM((NX, NZ, NY, 16, 2 * HD), bf),
            pltpu.VMEM((2 * NZ, NY, UNIT, HD), bf),
            pltpu.VMEM((GRP * 2 * ROWS, HD), bf),
            pltpu.VMEM((GRP * 2 * ROWS, ROWS), f32),
            pltpu.VMEM((GRP * 2 * ROWS, ROWS), f32),
            pltpu.VMEM((GRP * 2 * ROWS, HD), f32),
            pltpu.VMEM((8 * 64, 2 * HD), f32),
            pltpu.VMEM((ROWS, GRP * HD), bf),
            pltpu.VMEM((ROWS, GRP * HD), bf),
            pltpu.VMEM((4 * 64, 2 * HD), bf),
            pltpu.VMEM((4 * 64, 2 * HD), bf),
            dma((6,)),
            dma((6,)),
            dma((10, 7)),
            dma((10, 7)),
            dma((2, 6)),
            dma((2, 6)),
            dma((2, NZ // 2, NY)),
            dma((2, NZ // 2, NY)),
            dma((2, NZ // 2)),
            dma((2, NZ // 2)),
            dma((NZ + 1, NY - 1)),
            dma((NZ + 1, NY - 1)),
            dma((1,)),
        ],
        compiler_params=pltpu.CompilerParams(
            collective_id=0, has_side_effects=True, vmem_limit_bytes=56 << 20
        ),
        name="prefill",
    )(
        tokens[0],
        qkv_weight,
        q_gain.reshape(1, HD),
        k_gain.reshape(1, HD),
        inverse.reshape(1, half),
        page_table[0],
        block_ids[0],
        lengths,
    )
    return (attended[None], cache.reshape(1, 4, 64, 2 * HD))


def solution(mesh):
    in_specs = (
        P("req", "blk", None),
        P("req", "blk"),
        P("req"),
        P("req", None, None),
        P(("req", "blk"), None),
        P(),
        P(),
    )
    out_specs = (P("req", "blk", None), P("req", "blk", None, None))
    return jax.shard_map(body, mesh=mesh, in_specs=in_specs, out_specs=out_specs, check_vma=False)
```
